256 devices in a mesh: gx: 64 (over x, z, core), gy: 4 (over y).
Axes of the slice: x: 4, y: 4, z: 8, core: 2. Of those that a mesh axis runs over, the one named last changes fastest.
Arguments:
- amplitudes: float32 [2, 512, 128, 512], P(None, 'gx', None, 'gy'), may hold values from -6 to 6
- integrals: float32 [2, 32, 128, 128, 512], P(None, 'gy', None, 'gx'), may hold values from -0.09375 to 0.09375
- virt_count: int32 [8], replicated, may hold values from 24 to 128, as said below
- pair_irrep: int32 [8], replicated, may hold values from 0 to 7, as said below
- slab_index: int32 [1], replicated, may hold values from 0 to 15
- occ_energy: float32 [64], replicated, may hold values from -2 to -0.3
- virt_energy: float32 [512], replicated, may hold values from 0.1 to 3
Outputs:
- update: float32 [2, 512, 32, 128], P(None, 'gx', 'gy')
The draws below stay inside these ranges and needn't reach their ends.
Inputs may be any that keep to these rules, and one draw needn't show every extreme that they name: `virt_count`: entry k counts the virtual orbitals of irrep k; they sum to 512 and the largest is exactly 128. `pair_irrep`: a permutation of the irreps.
All inputs are finite; a program needn't handle non-finite values.
Results may differ from the reference program's by a relative error of at most 0.0001.
Values sent between devices are 32-bit elements; how exact they have to be, the bound alone decides.
No kernel may reach another device: no remote copies, remote signals or barrier semaphores. Data moves between devices by JAX's collectives and lax.ppermute only.
A program may use at most 64 MiB of HBM per device.

```python
import jax
import jax.numpy as jnp
from jax import lax

OCC = 64
VIRT = 512
SLAB = 32
IRREPS = 8
SYMS = 2
MAXIRR = 128
IJP = 512


def draw_virt_count(key, part):
    orbital_unit = VIRT // 64
    first_key, second_key = jax.random.split(jax.random.fold_in(key, 11))
    pair_low = jax.random.randint(first_key, (3,), 3 * orbital_unit, 10 * orbital_unit + 1).astype(jnp.int32)
    counts_list = jnp.concatenate([jnp.array([16 * orbital_unit, 9 * orbital_unit], jnp.int32), pair_low, (13 * orbital_unit - pair_low).astype(jnp.int32)])
    shuffle = jax.random.permutation(second_key, IRREPS)
    return counts_list[shuffle].astype(jnp.int32)


def draw_pair_irrep(key, part):
    shuffle = jax.random.permutation(jax.random.fold_in(key, 23), IRREPS)
    return shuffle.astype(jnp.int32)


def with_spikes(values, own_key, source, target, blocks, factor):
    owner, partner = [(jnp.arange(values.shape[position]) // (values.shape[position] // blocks)).reshape([-1 if axis == position else 1 for axis in range(values.ndim)]) for position in (source, target)]
    chosen = jax.random.permutation(own_key, blocks)[partner]
    strong = (owner == chosen) | (owner == (partner + blocks // 2) % blocks)
    return jnp.where(strong, factor * values, values)


def block_scale(rng, shape, pieces, least, largest):
    def one(dim, shards_of):
        heights = jax.random.uniform(jax.random.fold_in(jax.random.fold_in(rng, 6), dim), (shards_of,), jnp.float32, least / len(pieces), largest / len(pieces))
        return jnp.repeat(jnp.exp(heights), shape[dim] // shards_of).reshape((-1,) + (1,) * (len(shape) - dim - 1))

    level = one(*pieces[0])
    for cut in pieces[1:]:
        level = level * one(*cut)
    return level


def scatter_about(own_key, shape, deviation, most, cuts=(), held_as=jnp.bfloat16):
    values = deviation * jax.random.normal(own_key, shape, jnp.float32)
    if cuts:
        values = values * block_scale(own_key, shape, cuts, -0.22, 0.18)
    return jnp.clip(values, -most, most).astype(held_as)


def noise_with(key, extent, scale, most, shards, heavy, kind=jnp.bfloat16):
    values = scale * jax.random.normal(key, extent, jnp.float32)
    if shards:
        values = values * block_scale(key, extent, shards, -0.22, 0.18)
    return jnp.clip(with_spikes(values, jax.random.fold_in(key, 3), *heavy), -most, most).astype(kind)


def setup_inputs(seed: int = 0) -> dict:
    arg_keys = jax.random.split(jax.random.key(seed), 8)
    return {
        "amplitudes": scatter_about(arg_keys[0], (SYMS, IJP, MAXIRR, VIRT), 1.0, 6.0, ((1, 64), (3, 4)), jnp.float32),
        "integrals": noise_with(arg_keys[1], (SYMS, SLAB, MAXIRR, MAXIRR, VIRT), (VIRT * MAXIRR // 2) ** -0.5, 0.09375, ((1, 4), (3, 64)), (3, 2, 64, 4.0), jnp.float32),
        "virt_count": draw_virt_count(jax.random.fold_in(arg_keys[7], 71), 0),
        "pair_irrep": draw_pair_irrep(jax.random.fold_in(arg_keys[7], 71), 0),
        "slab_index": jax.random.randint(arg_keys[4], (1,), 0, VIRT // SLAB).astype(jnp.int32),
        "occ_energy": jnp.clip(jax.random.uniform(arg_keys[5], (OCC,), jnp.float32, -2.0, -0.3), -2.0, -0.3),
        "virt_energy": jnp.clip(jax.random.uniform(arg_keys[6], (VIRT,), jnp.float32, 0.1, 3.0), 0.1, 3.0),
    }


def irrep_of(positions, starts):
    return jnp.sum((positions[..., None] >= starts[1:]).astype(jnp.int32), axis=-1).astype(jnp.int32)


def lookup(entries, positions):
    picks = (positions[..., None] == jnp.arange(IRREPS, dtype=jnp.int32)).astype(entries.dtype)
    return jnp.sum(entries * picks, axis=-1)


def denominator_update(ladder, pair_rows, slab_rows, symmetry, slab_first, starts, virt_count, occ_energy, virt_energy):
    per_irrep = OCC // IRREPS
    occ_irrep = pair_rows // (per_irrep * per_irrep)
    first_occ = per_irrep * occ_irrep + (pair_rows % (per_irrep * per_irrep)) // per_irrep
    second_occ = per_irrep * jnp.bitwise_xor(occ_irrep, symmetry) + pair_rows % per_irrep
    occ_sum = jnp.take(occ_energy, first_occ) + jnp.take(occ_energy, second_occ)
    slab_virt = (SLAB * slab_first + slab_rows).astype(jnp.int32)
    partner = jnp.bitwise_xor(irrep_of(slab_virt, starts), symmetry)
    block_start = lookup(starts, partner)
    block_count = lookup(virt_count, partner)
    slot_range = jnp.arange(MAXIRR, dtype=jnp.int32)
    partner_orbital = jnp.clip(block_start[:, None] + slot_range[None, :], 0, VIRT - 1).astype(jnp.int32)
    slot_valid = slot_range[None, :] < block_count[:, None]
    denominator = occ_sum[:, None, None] - jnp.take(virt_energy, slab_virt)[None, :, None] - jnp.take(virt_energy, partner_orbital)[None]
    return jnp.where(slot_valid[None], ladder / denominator, jnp.zeros_like(ladder))


def reference(amplitudes, integrals, virt_count, pair_irrep, slab_index, occ_energy, virt_energy):
    starts = (jnp.cumsum(virt_count) - virt_count).astype(jnp.int32)
    slot_ids = jnp.arange(MAXIRR, dtype=jnp.int32)
    virt_ids = jnp.arange(VIRT, dtype=jnp.int32)
    base_irrep = irrep_of(virt_ids, starts)
    pair_rows = jnp.arange(IJP, dtype=jnp.int32)
    slab_rows = jnp.arange(SLAB, dtype=jnp.int32)
    updates = []
    for member in range(SYMS):
        symmetry = pair_irrep[member]
        partner = jnp.bitwise_xor(base_irrep, symmetry)
        slot_mask = slot_ids[:, None] < lookup(virt_count, partner)[None, :]
        masked = jnp.where(slot_mask[None], amplitudes[member], jnp.zeros_like(amplitudes[member]))
        ladder = lax.dot_general(masked.reshape(IJP, MAXIRR * VIRT), integrals[member].reshape(SLAB * MAXIRR, MAXIRR * VIRT), (((1,), (1,)), ((), ())), precision=lax.Precision.HIGHEST, preferred_element_type=jnp.float32)
        ladder = ladder.reshape(IJP, SLAB, MAXIRR)
        updates.append(denominator_update(ladder, pair_rows, slab_rows, symmetry, slab_index[0], starts, virt_count, occ_energy, virt_energy))
    return jnp.stack(updates)
```

```python
import jax
import jax.numpy as jnp
from jax import lax
from jax.sharding import Mesh
from jax.sharding import PartitionSpec as P

OCC = 64
VIRT = 512
SLAB = 32
IRREPS = 8
SYMS = 2
MAXIRR = 128
GX = ("x", "z", "c")


def irrep_of(positions, starts):
    return jnp.sum((positions[..., None] >= starts[1:]).astype(jnp.int32), axis=-1)


def lookup(entries, positions):
    picks = positions[..., None] == jnp.arange(IRREPS, dtype=jnp.int32)
    return jnp.sum(jnp.where(picks, entries, jnp.zeros_like(entries)), axis=-1)


def take(table, positions):
    picks = positions[..., None] == jnp.arange(table.shape[0], dtype=jnp.int32)
    return jnp.sum(jnp.where(picks, table, jnp.zeros_like(table)), axis=-1)


def denominators(pair_rows, slab_rows, symmetry, slab_first, starts, virt_count, occ, virt):
    per = OCC // IRREPS
    occ_irrep = pair_rows // (per * per)
    first = per * occ_irrep + pair_rows % (per * per) // per
    second = per * jnp.bitwise_xor(occ_irrep, symmetry) + pair_rows % per
    occ_sum = take(occ, first) + take(occ, second)
    slab_virt = SLAB * slab_first + slab_rows
    partner = jnp.bitwise_xor(irrep_of(slab_virt, starts), symmetry)
    slots = jnp.arange(MAXIRR, dtype=jnp.int32)
    orbital = jnp.clip(lookup(starts, partner)[:, None] + slots[None, :], 0, VIRT - 1)
    valid = slots[None, :] < lookup(virt_count, partner)[:, None]
    denominator = occ_sum[:, None, None] - take(virt, slab_virt)[None, :, None] - take(virt, orbital)[None]
    return denominator, jnp.broadcast_to(valid[None], denominator.shape)


def shift(value, axis, size, by):
    return lax.ppermute(value, axis, [(i, (i + by) % size) for i in range(size)])


def on_device(amplitudes, integrals, virt_count, pair_irrep, slab_index, occ_energy, virt_energy):
    starts = jnp.cumsum(virt_count) - virt_count
    handled = pair_irrep[:SYMS]
    core = lax.axis_index("c")
    y = lax.axis_index("y")
    chip = lax.axis_index("x") * 8 + lax.axis_index("z")
    block = chip * 2 + core

    send = amplitudes.reshape(2, 8, 32, 4, 128).transpose(2, 0, 3, 1, 4).reshape(64, 4, 8, 128)
    spread = lax.all_to_all(send, GX, split_axis=0, concat_axis=0, tiled=True)

    other = shift(lax.dynamic_index_in_dim(integrals, 1 - core, 0, False), "c", 2, 1)
    own = lax.dynamic_index_in_dim(integrals, core, 0, False)
    first = core == 0
    low = jnp.where(first, own, other)
    high = jnp.where(first, other, own)
    pieces = jnp.concatenate([low, high], axis=2)
    virt_ids = jnp.arange(VIRT, dtype=jnp.int32)
    partner = jnp.bitwise_xor(irrep_of(virt_ids, starts), handled[core])
    slot_ids = 4 * chip + jnp.arange(4, dtype=jnp.int32)
    valid = slot_ids[:, None] < lookup(virt_count, partner)[None, :]
    pieces = jnp.where(valid[None, None], pieces, jnp.zeros_like(pieces))

    up = shift(spread, "y", 4, 1)
    down = shift(spread, "y", 4, -1)
    half = 32
    far = jnp.concatenate([shift(up[:half], "y", 4, 1), shift(down[half:], "y", 4, -1)], axis=0)
    ladder = 0.0
    for hop, part in ((0, spread), (1, up), (-1, down), (2, far)):
        quarter = lax.dynamic_slice_in_dim(pieces, 128 * ((y - hop) % 4), 128, 3)
        ladder = ladder + lax.dot_general(
            part,
            quarter,
            (((1, 3), (2, 3)), ((), ())),
            precision=lax.Precision.HIGH,
            preferred_element_type=jnp.float32,
        )
    sums = lax.all_to_all(ladder.reshape(4, 16, 8, 8, 128), "x", 0, 0, tiled=True).sum(0)
    sums = lax.all_to_all(sums, ("z", "c"), 0, 0, tiled=True)
    sums = sums.reshape(8, 2, 8, 8, 128).sum(0)

    pair_rows = block * 8 + jnp.arange(8, dtype=jnp.int32)
    slab_rows = y * 8 + jnp.arange(8, dtype=jnp.int32)
    updates = []
    for member in range(SYMS):
        denominator, keep = denominators(
            pair_rows, slab_rows, handled[member], slab_index[0], starts, virt_count, occ_energy, virt_energy
        )
        updates.append(jnp.where(keep, sums[member] / denominator, jnp.zeros_like(denominator)))
    return jnp.stack(updates)


def solution(mesh):
    fine = Mesh(mesh.devices.reshape(4, 8, 2, 4), ("x", "z", "c", "y"))
    placed = (P(None, GX, None, "y"), P(None, "y", None, GX, None), P(), P(), P(), P(), P())
    return jax.shard_map(
        on_device, mesh=fine, in_specs=placed, out_specs=P(None, GX, "y", None), check_vma=False
    )
```

```python
import functools

import jax
import jax.numpy as jnp
from jax import lax
from jax.experimental import pallas as pl
from jax.experimental.pallas import tpu as pltpu
from jax.sharding import Mesh
from jax.sharding import PartitionSpec as P

OCC = 64
VIRT = 512
SLAB = 32
IRREPS = 8
SYMS = 2
MAXIRR = 128
GX = ("x", "z", "c")
HOPS = (0, 1, 3, 2)
STEP = 2


def irrep_of(positions, starts):
    return jnp.sum((positions[..., None] >= starts[1:]).astype(jnp.int32), axis=-1)


def lookup(entries, positions):
    picks = positions[..., None] == jnp.arange(IRREPS, dtype=jnp.int32)
    return jnp.sum(jnp.where(picks, entries, jnp.zeros_like(entries)), axis=-1)


def take(table, positions):
    picks = positions[..., None] == jnp.arange(table.shape[0], dtype=jnp.int32)
    return jnp.sum(jnp.where(picks, table, jnp.zeros_like(table)), axis=-1)


def denominators(pair_rows, slab_rows, symmetry, slab_first, starts, virt_count, occ, virt):
    per = OCC // IRREPS
    occ_irrep = pair_rows // (per * per)
    first = per * occ_irrep + pair_rows % (per * per) // per
    second = per * jnp.bitwise_xor(occ_irrep, symmetry) + pair_rows % per
    occ_sum = take(occ, first) + take(occ, second)
    slab_virt = SLAB * slab_first + slab_rows
    partner = jnp.bitwise_xor(irrep_of(slab_virt, starts), symmetry)
    slots = jnp.arange(MAXIRR, dtype=jnp.int32)
    orbital = jnp.clip(lookup(starts, partner)[:, None] + slots[None, :], 0, VIRT - 1)
    valid = slots[None, :] < lookup(virt_count, partner)[:, None]
    denominator = occ_sum[:, None, None] - take(virt, slab_virt)[None, :, None] - take(virt, orbital)[None]
    return denominator, jnp.broadcast_to(valid[None], denominator.shape)


def shift(value, axis, size, by):
    return lax.ppermute(value, axis, [(i, (i + by) % size) for i in range(size)])


def split(value):
    high = value.astype(jnp.bfloat16)
    return high, (value - high.astype(jnp.float32)).astype(jnp.bfloat16)


def three_pass(a_high, a_low, b_high, b_low):
    def dot(a, b):
        return lax.dot_general(a, b, (((1,), (1,)), ((), ())), preferred_element_type=jnp.float32)

    return dot(a_high, b_high) + (dot(a_high, b_low) + dot(a_low, b_high))


def masked_rows(part, slot, quarter, member, counts, irreps):
    e = 128 * quarter + lax.broadcasted_iota(jnp.int32, (1, 128), 1)
    symmetry = irreps[member]
    room = jnp.zeros((1, 128), jnp.int32)
    start = jnp.int32(0)
    for k in range(IRREPS):
        room = jnp.where(e >= start, counts[jnp.bitwise_xor(k, symmetry)], room)
        start = start + counts[k]
    return jnp.where(slot < room, part, 0.0)


def spread_rows(member, counts, irreps, part, k, hop, base, a_high, a_low):
    core, y = lax.axis_index("c"), lax.axis_index("y")
    chip = lax.axis_index("x") * 8 + lax.axis_index("z")
    quarter = lax.rem(y + 4 - hop, 4)
    for j in range(2):
        at = pl.multiple_of(base + 256 * jnp.bitwise_xor(core, k) + 128 * j, 128)
        for ahead in range(4):
            x = lax.rem(lax.axis_index("x") + ahead, 4)
            rows = part[pl.ds(8 * x, 8), j].reshape(64, 128)
            rows = masked_rows(rows, 4 * chip + 2 * k + j, quarter, member, counts, irreps)
            high, low = split(rows)
            a_high[64 * ahead : 64 * ahead + 64, pl.ds(at, 128)] = high
            a_low[64 * ahead : 64 * ahead + 64, pl.ds(at, 128)] = low


def near_kernel(member, counts, irreps, *refs):
    parts, (own, other, out, far_high, far_low, a_high, a_low, b_high, b_low, held, sems) = refs[:6], refs[6:]
    copies = [
        [pltpu.make_async_copy(source.at[member, n], held.at[k, n], sems.at[k, n]) for k, source in enumerate((own, other))]
        for n in range(8)
    ]
    for pair in copies:
        for copy in pair:
            copy.start()

    def load(first):
        for pair in copies[first : first + STEP]:
            for copy in pair:
                copy.wait()
        highs, lows = [], []
        for hop in HOPS:
            quarter = lax.rem(lax.axis_index("y") + 4 - hop, 4)
            for k in range(2):
                for j in range(2):
                    rows = [held[k, first + n, pl.ds(2 * quarter + j, 128, stride=8), :] for n in range(STEP)]
                    high, low = split(jnp.concatenate(rows, axis=0))
                    highs.append(high)
                    lows.append(low)
        rows = slice(128 * first, 128 * (first + STEP))
        b_high[rows, :] = jnp.concatenate(highs[:12], axis=1)
        b_low[rows, :] = jnp.concatenate(lows[:12], axis=1)
        far_high[rows, :] = jnp.concatenate(highs[12:], axis=1)
        far_low[rows, :] = jnp.concatenate(lows[12:], axis=1)

    for i in range(3):
        for k in range(2):
            spread_rows(member, counts, irreps, parts[2 * i + k], k, HOPS[i], 512 * i, a_high, a_low)
    for at in range(0, 8, STEP):
        load(at)
    out[...] = three_pass(b_high[...], b_low[...], a_high[...], a_low[...])


def far_kernel(member, counts, irreps, up, down, b_high, b_low, near, out0, out1, out2, out3, a_high, a_low):
    for k, part in enumerate((up, down)):
        spread_rows(member, counts, irreps, part, k, 2, 0, a_high, a_low)
    total = near[...] + three_pass(b_high[...], b_low[...], a_high[...], a_low[...])
    for n in range(8):
        part = total[128 * n : 128 * n + 128, :].T.reshape(4, 8, 8, 128)
        for ahead, out in enumerate((out0, out1, out2, out3)):
            out[:, n] = part[ahead]


SMEM = pl.BlockSpec(memory_space=pltpu.SMEM)
VMEM = pl.BlockSpec(memory_space=pltpu.VMEM)
HBM = pl.BlockSpec(memory_space=pltpu.HBM)


def near_product(member, counts, irreps, parts, own, other):
    return pl.pallas_call(
        functools.partial(near_kernel, member),
        in_specs=[SMEM, SMEM] + [VMEM] * 6 + [HBM, HBM],
        out_specs=[VMEM] * 3,
        out_shape=[
            jax.ShapeDtypeStruct((1024, 256), jnp.float32),
            jax.ShapeDtypeStruct((1024, 512), jnp.bfloat16),
            jax.ShapeDtypeStruct((1024, 512), jnp.bfloat16),
        ],
        scratch_shapes=[pltpu.VMEM((256, 1536), jnp.bfloat16)] * 2
        + [pltpu.VMEM((1024, 1536), jnp.bfloat16)] * 2
        + [pltpu.VMEM((2, 8, 1024, 128), jnp.float32), pltpu.SemaphoreType.DMA((2, 8))],
        compiler_params=pltpu.CompilerParams(vmem_limit_bytes=24 << 20),
        cost_estimate=pl.CostEstimate(flops=3 * 2 * 256 * 1024 * 1536, bytes_accessed=14 << 20, transcendentals=0),
    )(counts, irreps, *parts, own, other)


def far_product(member, counts, irreps, up, down, b_high, b_low, near):
    return pl.pallas_call(
        functools.partial(far_kernel, member),
        in_specs=[SMEM, SMEM] + [VMEM] * 5,
        out_specs=[VMEM] * 4,
        out_shape=[jax.ShapeDtypeStruct((8, 8, 8, 128), jnp.float32)] * 4,
        scratch_shapes=[pltpu.VMEM((256, 512), jnp.bfloat16)] * 2,
        compiler_params=pltpu.CompilerParams(vmem_limit_bytes=10 << 20),
        cost_estimate=pl.CostEstimate(flops=3 * 2 * 256 * 1024 * 512, bytes_accessed=5 << 20, transcendentals=0),
    )(counts, irreps, up, down, b_high, b_low, near)


def on_device(amplitudes, integrals, virt_count, pair_irrep, slab_index, occ_energy, virt_energy):
    starts = jnp.cumsum(virt_count) - virt_count
    handled = pair_irrep[:SYMS]
    core = lax.axis_index("c")
    y = lax.axis_index("y")
    block = (lax.axis_index("x") * 8 + lax.axis_index("z")) * 2 + core

    own = integrals.reshape(2, 8, 128, 2, 4, 128).transpose(0, 1, 2, 4, 3, 5).reshape(2, 8, 1024, 128)
    other = shift(own, "c", 2, 1)
    send = [amplitudes[g].reshape(8, 32, 4, 128).transpose(1, 2, 0, 3) for g in range(SYMS)]
    spreads = [lax.all_to_all(send[g], ("x", "z"), split_axis=0, concat_axis=0, tiled=True) for g in range(SYMS)]

    ladders = []
    for g in range(SYMS):
        low, high = spreads[g][:, :2], spreads[g][:, 2:]
        up_low, down_high = shift(low, "y", 4, 1), shift(high, "y", 4, -1)
        up_high, down_low = shift(high, "y", 4, 1), shift(low, "y", 4, -1)
        far_low, far_high = shift(up_low, "y", 4, 1), shift(down_high, "y", 4, -1)
        parts = (low, high, up_low, up_high, down_low, down_high)
        near, b_high, b_low = near_product(g, virt_count, pair_irrep, parts, own, other)
        ladders.append(far_product(g, virt_count, pair_irrep, far_low, far_high, b_high, b_low, near))

    updates = []
    for g in range(SYMS):
        mine, after, across, before = ladders[g]
        sums = mine + shift(after, "x", 4, 1) + shift(across, "x", 4, 2) + shift(before, "x", 4, -1)
        sums = lax.all_to_all(sums, "z", 0, 0, tiled=True).sum(0)

        pair_rows = block * 8 + jnp.arange(8, dtype=jnp.int32)
        slab_rows = y * 8 + jnp.arange(8, dtype=jnp.int32)
        denominator, keep = denominators(
            pair_rows, slab_rows, handled[g], slab_index[0], starts, virt_count, occ_energy, virt_energy
        )
        ladder = sums.transpose(1, 0, 2)
        updates.append(jnp.where(keep, ladder / denominator, jnp.zeros_like(denominator)))
    return jnp.stack(updates)


def solution(mesh):
    fine = Mesh(mesh.devices.reshape(4, 8, 2, 4), ("x", "z", "c", "y"))
    placed = (P(None, GX, None, "y"), P(None, "y", None, GX, None), P(), P(), P(), P(), P())
    return jax.shard_map(
        on_device, mesh=fine, in_specs=placed, out_specs=P(None, GX, "y", None), check_vma=False
    )
```

```python
import functools

import jax
import jax.numpy as jnp
from jax import lax
from jax.experimental import pallas as pl
from jax.experimental.pallas import tpu as pltpu
from jax.sharding import Mesh
from jax.sharding import PartitionSpec as P

OCC = 64
VIRT = 512
SLAB = 32
IRREPS = 8
SYMS = 2
MAXIRR = 128
GX = ("x", "z", "c")
HOPS = (0, 1, 3, 2)
STEP = 2


def irrep_of(positions, starts):
    return jnp.sum((positions[..., None] >= starts[1:]).astype(jnp.int32), axis=-1)


def lookup(entries, positions):
    picks = positions[..., None] == jnp.arange(IRREPS, dtype=jnp.int32)
    return jnp.sum(jnp.where(picks, entries, jnp.zeros_like(entries)), axis=-1)


def take(table, positions):
    picks = positions[..., None] == jnp.arange(table.shape[0], dtype=jnp.int32)
    return jnp.sum(jnp.where(picks, table, jnp.zeros_like(table)), axis=-1)


def denominators(pair_rows, slab_rows, symmetry, slab_first, starts, virt_count, occ, virt):
    per = OCC // IRREPS
    occ_irrep = pair_rows // (per * per)
    first = per * occ_irrep + pair_rows % (per * per) // per
    second = per * jnp.bitwise_xor(occ_irrep, symmetry) + pair_rows % per
    occ_sum = take(occ, first) + take(occ, second)
    slab_virt = SLAB * slab_first + slab_rows
    partner = jnp.bitwise_xor(irrep_of(slab_virt, starts), symmetry)
    slots = jnp.arange(MAXIRR, dtype=jnp.int32)
    orbital = jnp.clip(lookup(starts, partner)[:, None] + slots[None, :], 0, VIRT - 1)
    valid = slots[None, :] < lookup(virt_count, partner)[:, None]
    denominator = occ_sum[:, None, None] - take(virt, slab_virt)[None, :, None] - take(virt, orbital)[None]
    return denominator, jnp.broadcast_to(valid[None], denominator.shape)


def shift(value, axis, size, by):
    return lax.ppermute(value, axis, [(i, (i + by) % size) for i in range(size)])


def split(value):
    high = value.astype(jnp.bfloat16)
    return high, (value - high.astype(jnp.float32)).astype(jnp.bfloat16)


def three_pass(a_high, a_low, b_high, b_low):
    def dot(a, b):
        return lax.dot_general(a, b, (((1,), (1,)), ((), ())), preferred_element_type=jnp.float32)

    return dot(a_high, b_high) + (dot(a_high, b_low) + dot(a_low, b_high))


def masked_rows(part, slot, quarter, member, counts, irreps):
    e = 128 * quarter + lax.broadcasted_iota(jnp.int32, (1, 128), 1)
    symmetry = irreps[member]
    room = jnp.zeros((1, 128), jnp.int32)
    start = jnp.int32(0)
    for k in range(IRREPS):
        room = jnp.where(e >= start, counts[jnp.bitwise_xor(k, symmetry)], room)
        start = start + counts[k]
    return jnp.where(slot < room, part, 0.0)


def spread_rows(member, counts, irreps, part, k, hop, base, a_high, a_low):
    core, y = lax.axis_index("c"), lax.axis_index("y")
    chip = lax.axis_index("x") * 8 + lax.axis_index("z")
    quarter = lax.rem(y + 4 - hop, 4)
    for j in range(2):
        at = pl.multiple_of(base + 256 * jnp.bitwise_xor(core, k) + 128 * j, 128)
        for ahead in range(4):
            x = lax.rem(lax.axis_index("x") + ahead, 4)
            rows = part[pl.ds(8 * x, 8), j].reshape(64, 128)
            rows = masked_rows(rows, 4 * chip + 2 * k + j, quarter, member, counts, irreps)
            high, low = split(rows)
            a_high[64 * ahead : 64 * ahead + 64, pl.ds(at, 128)] = high
            a_low[64 * ahead : 64 * ahead + 64, pl.ds(at, 128)] = low


def near_kernel(member, counts, irreps, *refs):
    parts, (own, other, out, far_high, far_low, a_high, a_low, b_high, b_low, held, sems) = refs[:6], refs[6:]
    copies = [
        [pltpu.make_async_copy(source.at[member, n], held.at[k, n], sems.at[k, n]) for k, source in enumerate((own, other))]
        for n in range(8)
    ]
    for pair in copies:
        for copy in pair:
            copy.start()

    def load(first):
        for pair in copies[first : first + STEP]:
            for copy in pair:
                copy.wait()
        highs, lows = [], []
        for hop in HOPS:
            quarter = lax.rem(lax.axis_index("y") + 4 - hop, 4)
            for k in range(2):
                for j in range(2):
                    rows = [held[k, first + n, pl.ds(2 * quarter + j, 128, stride=8), :] for n in range(STEP)]
                    high, low = split(jnp.concatenate(rows, axis=0))
                    highs.append(high)
                    lows.append(low)
        rows = slice(128 * first, 128 * (first + STEP))
        b_high[rows, :] = jnp.concatenate(highs[:12], axis=1)
        b_low[rows, :] = jnp.concatenate(lows[:12], axis=1)
        far_high[rows, :] = jnp.concatenate(highs[12:], axis=1)
        far_low[rows, :] = jnp.concatenate(lows[12:], axis=1)

    for i in range(3):
        for k in range(2):
            spread_rows(member, counts, irreps, parts[2 * i + k], k, HOPS[i], 512 * i, a_high, a_low)
    for at in range(0, 8, STEP):
        load(at)
    out[...] = three_pass(b_high[...], b_low[...], a_high[...], a_low[...])


def far_kernel(member, counts, irreps, up, down, b_high, b_low, near, out0, out1, out2, out3, a_high, a_low):
    for k, part in enumerate((up, down)):
        spread_rows(member, counts, irreps, part, k, 2, 0, a_high, a_low)
    total = near[...] + three_pass(b_high[...], b_low[...], a_high[...], a_low[...])
    for n in range(8):
        part = total[128 * n : 128 * n + 128, :].T.reshape(4, 8, 8, 128)
        for ahead, out in enumerate((out0, out1, out2, out3)):
            out[:, n] = part[ahead]


SMEM = pl.BlockSpec(memory_space=pltpu.SMEM)
VMEM = pl.BlockSpec(memory_space=pltpu.VMEM)
HBM = pl.BlockSpec(memory_space=pltpu.HBM)


def near_product(member, counts, irreps, parts, own, other):
    return pl.pallas_call(
        functools.partial(near_kernel, member),
        in_specs=[SMEM, SMEM] + [VMEM] * 6 + [HBM, HBM],
        out_specs=[VMEM] * 3,
        out_shape=[
            jax.ShapeDtypeStruct((1024, 256), jnp.float32),
            jax.ShapeDtypeStruct((1024, 512), jnp.bfloat16),
            jax.ShapeDtypeStruct((1024, 512), jnp.bfloat16),
        ],
        scratch_shapes=[pltpu.VMEM((256, 1536), jnp.bfloat16)] * 2
        + [pltpu.VMEM((1024, 1536), jnp.bfloat16)] * 2
        + [pltpu.VMEM((2, 8, 1024, 128), jnp.float32), pltpu.SemaphoreType.DMA((2, 8))],
        compiler_params=pltpu.CompilerParams(vmem_limit_bytes=46 << 20),
        cost_estimate=pl.CostEstimate(flops=3 * 2 * 256 * 1024 * 1536, bytes_accessed=14 << 20, transcendentals=0),
    )(counts, irreps, *parts, own, other)


def far_product(member, counts, irreps, up, down, b_high, b_low, near):
    return pl.pallas_call(
        functools.partial(far_kernel, member),
        in_specs=[SMEM, SMEM] + [VMEM] * 5,
        out_specs=[VMEM] * 4,
        out_shape=[jax.ShapeDtypeStruct((8, 8, 8, 128), jnp.float32)] * 4,
        scratch_shapes=[pltpu.VMEM((256, 512), jnp.bfloat16)] * 2,
        compiler_params=pltpu.CompilerParams(vmem_limit_bytes=10 << 20),
        cost_estimate=pl.CostEstimate(flops=3 * 2 * 256 * 1024 * 512, bytes_accessed=5 << 20, transcendentals=0),
    )(counts, irreps, up, down, b_high, b_low, near)


def on_device(amplitudes, integrals, virt_count, pair_irrep, slab_index, occ_energy, virt_energy):
    starts = jnp.cumsum(virt_count) - virt_count
    handled = pair_irrep[:SYMS]
    core = lax.axis_index("c")
    y = lax.axis_index("y")
    block = (lax.axis_index("x") * 8 + lax.axis_index("z")) * 2 + core

    own = integrals.reshape(2, 8, 128, 2, 4, 128).transpose(0, 1, 2, 4, 3, 5).reshape(2, 8, 1024, 128)
    other = shift(own, "c", 2, 1)
    send = [amplitudes[g].reshape(8, 32, 4, 128).transpose(1, 2, 0, 3) for g in range(SYMS)]
    spreads = [lax.all_to_all(send[g], ("x", "z"), split_axis=0, concat_axis=0, tiled=True) for g in range(SYMS)]

    ladders = []
    for g in range(SYMS):
        low, high = spreads[g][:, :2], spreads[g][:, 2:]
        up_low, down_high = shift(low, "y", 4, 1), shift(high, "y", 4, -1)
        up_high, down_low = shift(high, "y", 4, 1), shift(low, "y", 4, -1)
        far_low, far_high = shift(up_low, "y", 4, 1), shift(down_high, "y", 4, -1)
        parts = (low, high, up_low, up_high, down_low, down_high)
        near, b_high, b_low = near_product(g, virt_count, pair_irrep, parts, own, other)
        ladders.append(far_product(g, virt_count, pair_irrep, far_low, far_high, b_high, b_low, near))

    sums = []
    for mine, after, across, before in ladders:
        sums.append(mine + shift(after, "x", 4, 1) + shift(across, "x", 4, 2) + shift(before, "x", 4, -1))
    totals = lax.all_to_all(jnp.stack(sums, axis=1), "z", 0, 0, tiled=True).sum(0)

    updates = []
    for g in range(SYMS):
        pair_rows = block * 8 + jnp.arange(8, dtype=jnp.int32)
        slab_rows = y * 8 + jnp.arange(8, dtype=jnp.int32)
        denominator, keep = denominators(
            pair_rows, slab_rows, handled[g], slab_index[0], starts, virt_count, occ_energy, virt_energy
        )
        ladder = totals[g].transpose(1, 0, 2)
        updates.append(jnp.where(keep, ladder / denominator, jnp.zeros_like(denominator)))
    return jnp.stack(updates)


def solution(mesh):
    fine = Mesh(mesh.devices.reshape(4, 8, 2, 4), ("x", "z", "c", "y"))
    placed = (P(None, GX, None, "y"), P(None, "y", None, GX, None), P(), P(), P(), P(), P())
    return jax.shard_map(
        on_device, mesh=fine, in_specs=placed, out_specs=P(None, GX, "y", None), check_vma=False
    )
```

```python
import functools

import jax
import jax.numpy as jnp
from jax import lax
from jax.experimental import pallas as pl
from jax.experimental.pallas import tpu as pltpu
from jax.sharding import Mesh
from jax.sharding import PartitionSpec as P

OCC = 64
VIRT = 512
SLAB = 32
IRREPS = 8
SYMS = 2
MAXIRR = 128
GX = ("x", "z", "c")
HOPS = (0, 1, 3, 2)
STEP = 1


def irrep_of(positions, starts):
    return jnp.sum((positions[..., None] >= starts[1:]).astype(jnp.int32), axis=-1)


def lookup(entries, positions):
    picks = positions[..., None] == jnp.arange(IRREPS, dtype=jnp.int32)
    return jnp.sum(jnp.where(picks, entries, jnp.zeros_like(entries)), axis=-1)


def take(table, positions):
    picks = positions[..., None] == jnp.arange(table.shape[0], dtype=jnp.int32)
    return jnp.sum(jnp.where(picks, table, jnp.zeros_like(table)), axis=-1)


def denominators(pair_rows, slab_rows, symmetry, slab_first, starts, virt_count, occ, virt):
    per = OCC // IRREPS
    occ_irrep = pair_rows // (per * per)
    first = per * occ_irrep + pair_rows % (per * per) // per
    second = per * jnp.bitwise_xor(occ_irrep, symmetry) + pair_rows % per
    occ_sum = take(occ, first) + take(occ, second)
    slab_virt = SLAB * slab_first + slab_rows
    partner = jnp.bitwise_xor(irrep_of(slab_virt, starts), symmetry)
    slots = jnp.arange(MAXIRR, dtype=jnp.int32)
    orbital = jnp.clip(lookup(starts, partner)[:, None] + slots[None, :], 0, VIRT - 1)
    valid = slots[None, :] < lookup(virt_count, partner)[:, None]
    denominator = occ_sum[:, None, None] - take(virt, slab_virt)[None, :, None] - take(virt, orbital)[None]
    return denominator, jnp.broadcast_to(valid[None], denominator.shape)


def shift(value, axis, size, by):
    return lax.ppermute(value, axis, [(i, (i + by) % size) for i in range(size)])


def split(value):
    high = value.astype(jnp.bfloat16)
    return high, (value - high.astype(jnp.float32)).astype(jnp.bfloat16)


def three_pass(a_high, a_low, b_high, b_low):
    def dot(a, b):
        return lax.dot_general(a, b, (((1,), (1,)), ((), ())), preferred_element_type=jnp.float32)

    return dot(a_high, b_high) + (dot(a_high, b_low) + dot(a_low, b_high))


def masked_rows(part, slot, quarter, member, counts, irreps):
    e = 128 * quarter + lax.broadcasted_iota(jnp.int32, (1, 128), 1)
    symmetry = irreps[member]
    room = jnp.zeros((1, 128), jnp.int32)
    start = jnp.int32(0)
    for k in range(IRREPS):
        room = jnp.where(e >= start, counts[jnp.bitwise_xor(k, symmetry)], room)
        start = start + counts[k]
    return jnp.where(slot < room, part, 0.0)


def spread_rows(member, counts, irreps, part, k, hop, base, a_high, a_low):
    core, y = lax.axis_index("c"), lax.axis_index("y")
    chip = lax.axis_index("x") * 8 + lax.axis_index("z")
    quarter = lax.rem(y + 4 - hop, 4)
    for j in range(2):
        at = pl.multiple_of(base + 256 * jnp.bitwise_xor(core, k) + 128 * j, 128)
        for ahead in range(4):
            x = lax.rem(lax.axis_index("x") + ahead, 4)
            rows = part[pl.ds(8 * x, 8), j].reshape(64, 128)
            rows = masked_rows(rows, 4 * chip + 2 * k + j, quarter, member, counts, irreps)
            high, low = split(rows)
            a_high[64 * ahead : 64 * ahead + 64, pl.ds(at, 128)] = high
            a_low[64 * ahead : 64 * ahead + 64, pl.ds(at, 128)] = low


def near_kernel(member, counts, irreps, *refs):
    parts, (own, other, out, far_high, far_low, a_high, a_low, b_high, b_low, held, sems) = refs[:6], refs[6:]
    copies = [
        [pltpu.make_async_copy(source.at[member, n], held.at[k, n], sems.at[k, n]) for k, source in enumerate((own, other))]
        for n in range(8)
    ]
    for pair in copies:
        for copy in pair:
            copy.start()

    def load(first):
        for pair in copies[first : first + STEP]:
            for copy in pair:
                copy.wait()
        highs, lows = [], []
        for hop in HOPS:
            quarter = lax.rem(lax.axis_index("y") + 4 - hop, 4)
            for k in range(2):
                for j in range(2):
                    rows = [held[k, first + n, pl.ds(2 * quarter + j, 128, stride=8), :] for n in range(STEP)]
                    high, low = split(jnp.concatenate(rows, axis=0))
                    highs.append(high)
                    lows.append(low)
        rows = slice(128 * first, 128 * (first + STEP))
        b_high[rows, :] = jnp.concatenate(highs[:12], axis=1)
        b_low[rows, :] = jnp.concatenate(lows[:12], axis=1)
        far_high[rows, :] = jnp.concatenate(highs[12:], axis=1)
        far_low[rows, :] = jnp.concatenate(lows[12:], axis=1)

    for i in range(3):
        for k in range(2):
            spread_rows(member, counts, irreps, parts[2 * i + k], k, HOPS[i], 512 * i, a_high, a_low)
    for at in range(0, 8, STEP):
        load(at)
    out[...] = three_pass(b_high[...], b_low[...], a_high[...], a_low[...])


def far_kernel(member, counts, irreps, up, down, b_high, b_low, near, out0, out1, out2, out3, a_high, a_low):
    for k, part in enumerate((up, down)):
        spread_rows(member, counts, irreps, part, k, 2, 0, a_high, a_low)
    total = near[...] + three_pass(b_high[...], b_low[...], a_high[...], a_low[...])
    for n in range(8):
        part = total[128 * n : 128 * n + 128, :].T.reshape(4, 8, 8, 128)
        for ahead, out in enumerate((out0, out1, out2, out3)):
            out[:, n] = part[ahead]


SMEM = pl.BlockSpec(memory_space=pltpu.SMEM)
VMEM = pl.BlockSpec(memory_space=pltpu.VMEM)
HBM = pl.BlockSpec(memory_space=pltpu.HBM)


def near_product(member, counts, irreps, parts, own, other):
    return pl.pallas_call(
        functools.partial(near_kernel, member),
        in_specs=[SMEM, SMEM] + [VMEM] * 6 + [HBM, HBM],
        out_specs=[VMEM] * 3,
        out_shape=[
            jax.ShapeDtypeStruct((1024, 256), jnp.float32),
            jax.ShapeDtypeStruct((1024, 512), jnp.bfloat16),
            jax.ShapeDtypeStruct((1024, 512), jnp.bfloat16),
        ],
        scratch_shapes=[pltpu.VMEM((256, 1536), jnp.bfloat16)] * 2
        + [pltpu.VMEM((1024, 1536), jnp.bfloat16)] * 2
        + [pltpu.VMEM((2, 8, 1024, 128), jnp.float32), pltpu.SemaphoreType.DMA((2, 8))],
        compiler_params=pltpu.CompilerParams(vmem_limit_bytes=46 << 20),
        cost_estimate=pl.CostEstimate(flops=3 * 2 * 256 * 1024 * 1536, bytes_accessed=14 << 20, transcendentals=0),
    )(counts, irreps, *parts, own, other)


def far_product(member, counts, irreps, up, down, b_high, b_low, near):
    return pl.pallas_call(
        functools.partial(far_kernel, member),
        in_specs=[SMEM, SMEM] + [VMEM] * 5,
        out_specs=[VMEM] * 4,
        out_shape=[jax.ShapeDtypeStruct((8, 8, 8, 128), jnp.float32)] * 4,
        scratch_shapes=[pltpu.VMEM((256, 512), jnp.bfloat16)] * 2,
        compiler_params=pltpu.CompilerParams(vmem_limit_bytes=10 << 20),
        cost_estimate=pl.CostEstimate(flops=3 * 2 * 256 * 1024 * 512, bytes_accessed=5 << 20, transcendentals=0),
    )(counts, irreps, up, down, b_high, b_low, near)


def on_device(amplitudes, integrals, virt_count, pair_irrep, slab_index, occ_energy, virt_energy):
    starts = jnp.cumsum(virt_count) - virt_count
    handled = pair_irrep[:SYMS]
    core = lax.axis_index("c")
    y = lax.axis_index("y")
    block = (lax.axis_index("x") * 8 + lax.axis_index("z")) * 2 + core

    own = integrals.reshape(2, 8, 128, 2, 4, 128).transpose(0, 1, 2, 4, 3, 5).reshape(2, 8, 1024, 128)
    other = shift(own, "c", 2, 1)
    send = [amplitudes[g].reshape(8, 32, 4, 128).transpose(1, 2, 0, 3) for g in range(SYMS)]
    spreads = [lax.all_to_all(send[g], ("x", "z"), split_axis=0, concat_axis=0, tiled=True) for g in range(SYMS)]

    ladders = []
    for g in range(SYMS):
        low, high = spreads[g][:, :2], spreads[g][:, 2:]
        up_low, down_high = shift(low, "y", 4, 1), shift(high, "y", 4, -1)
        up_high, down_low = shift(high, "y", 4, 1), shift(low, "y", 4, -1)
        far_low, far_high = shift(up_low, "y", 4, 1), shift(down_high, "y", 4, -1)
        parts = (low, high, up_low, up_high, down_low, down_high)
        near, b_high, b_low = near_product(g, virt_count, pair_irrep, parts, own, other)
        ladders.append(far_product(g, virt_count, pair_irrep, far_low, far_high, b_high, b_low, near))

    sums = []
    for mine, after, across, before in ladders:
        sums.append(mine + shift(after, "x", 4, 1) + shift(across, "x", 4, 2) + shift(before, "x", 4, -1))
    totals = lax.all_to_all(jnp.stack(sums, axis=1), "z", 0, 0, tiled=True).sum(0)

    updates = []
    for g in range(SYMS):
        pair_rows = block * 8 + jnp.arange(8, dtype=jnp.int32)
        slab_rows = y * 8 + jnp.arange(8, dtype=jnp.int32)
        denominator, keep = denominators(
            pair_rows, slab_rows, handled[g], slab_index[0], starts, virt_count, occ_energy, virt_energy
        )
        ladder = totals[g].transpose(1, 0, 2)
        updates.append(jnp.where(keep, ladder / denominator, jnp.zeros_like(denominator)))
    return jnp.stack(updates)


def solution(mesh):
    fine = Mesh(mesh.devices.reshape(4, 8, 2, 4), ("x", "z", "c", "y"))
    placed = (P(None, GX, None, "y"), P(None, "y", None, GX, None), P(), P(), P(), P(), P())
    return jax.shard_map(
        on_device, mesh=fine, in_specs=placed, out_specs=P(None, GX, "y", None), check_vma=False
    )
```
